32 devices in a mesh: dp: 4 (over x, core), seq: 4 (over z), shard: 2 (over y).
Axes of the slice: x: 2, y: 2, z: 4, core: 2. Of those that a mesh axis runs over, the one named last changes fastest.
Arguments:
- layer_input: bfloat16 [8, 2048, 1024], P(('dp', 'shard'), 'seq'), may hold values from -6 to 6
- cond_table: bfloat16 [8, 1024], replicated, may hold values from -3 to 3
- window_bucket: int32 [8], P(('dp', 'shard')), may hold values from 0 to 7, as said below
- window_blocks: int32 [8], P(('dp', 'shard')), may hold values from 1 to 16, as said below
- cotangent: bfloat16 [8, 2048, 1024], P(('dp', 'shard'), 'seq'), may hold values from -6 to 6
- ln1_gain: float32 [1024], P(('dp', 'seq', 'shard')), may hold values from 0.25 to 1.75
- ln1_bias: float32 [1024], P(('dp', 'seq', 'shard')), may hold values from -2 to 2
- qkv_weight: float32 [1024, 3072], P(('dp', 'seq', 'shard')), may hold values from -0.1875 to 0.1875
- query_bias: float32 [1024], P(('dp', 'seq', 'shard')), may hold values from -2 to 2
- value_bias: float32 [1024], P(('dp', 'seq', 'shard')), may hold values from -2 to 2
- out_weight: float32 [1024, 1024], P(('dp', 'seq', 'shard')), may hold values from -0.75 to 0.75
- out_bias: float32 [1024], P(('dp', 'seq', 'shard')), may hold values from -2 to 2
- ln2_gain: float32 [1024], P(('dp', 'seq', 'shard')), may hold values from 0.25 to 1.75
- ln2_bias: float32 [1024], P(('dp', 'seq', 'shard')), may hold values from -2 to 2
- fc_weight: float32 [1024, 4096], P(('dp', 'seq', 'shard')), may hold values from -0.1875 to 0.1875
- fc_bias: float32 [4096], P(('dp', 'seq', 'shard')), may hold values from -2 to 2
- proj_weight: float32 [4096, 1024], P(('dp', 'seq', 'shard')), may hold values from -0.09375 to 0.09375
- proj_bias: float32 [1024], P(('dp', 'seq', 'shard')), may hold values from -2 to 2
Outputs:
- layer_output: bfloat16 [8, 2048, 1024], P(('dp', 'shard'), 'seq')
- input_grad: float32 [8, 2048, 1024], P(('dp', 'shard'), 'seq')
- ln1_gain_grad: float32 [1024], P(('dp', 'seq', 'shard'))
- ln1_bias_grad: float32 [1024], P(('dp', 'seq', 'shard'))
- qkv_weight_grad: float32 [1024, 3072], P(('dp', 'seq', 'shard'))
- query_bias_grad: float32 [1024], P(('dp', 'seq', 'shard'))
- value_bias_grad: float32 [1024], P(('dp', 'seq', 'shard'))
- out_weight_grad: float32 [1024, 1024], P(('dp', 'seq', 'shard'))
- out_bias_grad: float32 [1024], P(('dp', 'seq', 'shard'))
- ln2_gain_grad: float32 [1024], P(('dp', 'seq', 'shard'))
- ln2_bias_grad: float32 [1024], P(('dp', 'seq', 'shard'))
- fc_weight_grad: float32 [1024, 4096], P(('dp', 'seq', 'shard'))
- fc_bias_grad: float32 [4096], P(('dp', 'seq', 'shard'))
- proj_weight_grad: float32 [4096, 1024], P(('dp', 'seq', 'shard'))
- proj_bias_grad: float32 [1024], P(('dp', 'seq', 'shard'))
The draws below stay inside these ranges and needn't reach their ends.
Inputs may be any that keep to these rules, and one draw needn't show every extreme that they name: `window_bucket`: some window has bucket 0 and some other bucket 8 - 1. `window_blocks`: some window has 16 live rows and some other has 1.
All inputs are finite; a program needn't handle non-finite values.
Results may differ from the reference program's by a relative error of at most 0.012.
The reference program's roundings to bfloat16 on the way count: a program that leaves them out, or rounds other values in their place, can miss the bound.
Values may be sent and summed in bfloat16 or wider, within the bound.
A program may use at most 192 MiB of HBM per device.

```python
import jax
import jax.numpy as jnp
from jax import lax

D = 1024
HEADS = 16
HEAD_DIM = 64
FF = 4096
ROW = 128
WIN_BLOCKS = 16
BUCKETS = 8
LEN = 2048
WINDOWS = 8


def draw_window_bucket(key, part):
    first, second, third = jax.random.split(jax.random.fold_in(key, 11), 3)
    chosen = jax.random.randint(first, (WINDOWS,), 0, BUCKETS)
    high_at = jax.random.randint(second, (), 0, WINDOWS)
    low_at = (high_at + 1 + jax.random.randint(third, (), 0, WINDOWS - 1)) % WINDOWS
    places = jnp.arange(WINDOWS)
    chosen = jnp.where(places == high_at, BUCKETS - 1, chosen)
    chosen = jnp.where(places == low_at, 0, chosen)
    return chosen.astype(jnp.int32)


def draw_window_blocks(key, part):
    first, second, third = jax.random.split(jax.random.fold_in(key, 23), 3)
    counts = jax.random.randint(first, (WINDOWS,), 1, WIN_BLOCKS + 1)
    full_at = jax.random.randint(second, (), 0, WINDOWS)
    short_at = (full_at + 1 + jax.random.randint(third, (), 0, WINDOWS - 1)) % WINDOWS
    places = jnp.arange(WINDOWS)
    counts = jnp.where(places == full_at, WIN_BLOCKS, counts)
    counts = jnp.where(places == short_at, 1, counts)
    return counts.astype(jnp.int32)


def with_spikes(array, stream_key, source, target, parts, factor):
    owner, partner = [(jnp.arange(array.shape[dim]) // (array.shape[dim] // parts)).reshape([-1 if axis == dim else 1 for axis in range(array.ndim)]) for dim in (source, target)]
    chosen = jax.random.permutation(stream_key, parts)[partner]
    strong = (owner == chosen) | (owner == (partner + parts // 2) % parts)
    return jnp.where(strong, factor * array, array)


def block_levels(key, shape, shards, low, largest):
    gain, own = 1.0, jax.random.fold_in(key, 6)
    for position, shards_of in shards:
        steps = jnp.exp(jax.random.uniform(jax.random.fold_in(own, position), (shards_of,), jnp.float32, low / len(shards), largest / len(shards)))
        gain = gain * jnp.repeat(steps, shape[position] // shards_of).reshape([-1 if axis == position else 1 for axis in range(len(shape))])
    return gain


def scatter_about(rng, shape, deviation, bound, pieces=(), kind=jnp.bfloat16):
    result = deviation * jax.random.normal(rng, shape, jnp.float32)
    if pieces:
        result = result * block_levels(rng, shape, pieces, -0.22, 0.18)
    return jnp.clip(result, -bound, bound).astype(kind)


def noise_with(stream_key, extent, scale, limit, cuts, heavy, kind=jnp.bfloat16):
    drawn = scale * jax.random.normal(stream_key, extent, jnp.float32)
    if cuts:
        drawn = drawn * block_levels(stream_key, extent, cuts, -0.22, 0.18)
    return jnp.clip(with_spikes(drawn, jax.random.fold_in(stream_key, 3), *heavy), -limit, limit).astype(kind)


def setup_inputs(seed: int = 0) -> dict:
    key_of = jax.random.split(jax.random.key(seed), 19)
    layer_input = scatter_about(key_of[0], (WINDOWS, LEN, D), 1.0, 6.0, ((0, 8), (1, 4)))
    cond_table = scatter_about(key_of[1], (BUCKETS, D), 0.5, 3.0)
    window_bucket = draw_window_bucket(jax.random.fold_in(key_of[18], 71), 0)
    window_blocks = draw_window_blocks(jax.random.fold_in(key_of[18], 71), 0)
    cotangent = noise_with(key_of[4], (WINDOWS, LEN, D), 1.0, 6.0, ((0, 8), (1, 4)), (1, 2, 4, 2.0))
    ln1_gain = jnp.clip(1.0 + 0.15 * jax.random.normal(key_of[5], (D,), jnp.float32), 0.25, 1.75)
    ln1_bias = scatter_about(key_of[6], (D,), 0.3, 2.0, ((0, 32),), jnp.float32)
    qkv_weight = scatter_about(key_of[7], (D, 3 * D), D ** -0.5, 0.1875, ((0, 32),), jnp.float32)
    query_bias = scatter_about(key_of[8], (D,), 0.3, 2.0, ((0, 32),), jnp.float32)
    value_bias = scatter_about(key_of[9], (D,), 0.3, 2.0, ((0, 32),), jnp.float32)
    out_weight = scatter_about(key_of[10], (D, D), (D // 16) ** -0.5, 0.75, ((0, 32),), jnp.float32)
    out_bias = scatter_about(key_of[11], (D,), 0.3, 2.0, ((0, 32),), jnp.float32)
    ln2_gain = jnp.clip(1.0 + 0.15 * jax.random.normal(key_of[12], (D,), jnp.float32), 0.25, 1.75)
    ln2_bias = scatter_about(key_of[13], (D,), 0.3, 2.0, ((0, 32),), jnp.float32)
    fc_weight = scatter_about(key_of[14], (D, FF), D ** -0.5, 0.1875, ((0, 32),), jnp.float32)
    fc_bias = scatter_about(key_of[15], (FF,), 0.3, 2.0, ((0, 32),), jnp.float32)
    proj_weight = scatter_about(key_of[16], (FF, D), FF ** -0.5, 0.09375, ((0, 32),), jnp.float32)
    proj_bias = scatter_about(key_of[17], (D,), 0.3, 2.0, ((0, 32),), jnp.float32)
    return dict(layer_input=layer_input, cond_table=cond_table, window_bucket=window_bucket, window_blocks=window_blocks, cotangent=cotangent, ln1_gain=ln1_gain, ln1_bias=ln1_bias, qkv_weight=qkv_weight, query_bias=query_bias, value_bias=value_bias, out_weight=out_weight, out_bias=out_bias, ln2_gain=ln2_gain, ln2_bias=ln2_bias, fc_weight=fc_weight, fc_bias=fc_bias, proj_weight=proj_weight, proj_bias=proj_bias)


@jax.custom_vjp
def low(v):
    return lax.optimization_barrier(v.astype(jnp.bfloat16)).astype(jnp.float32)

@jax.custom_vjp
def low_back(v):
    return v

def low_keep(v):
    return (low(v), None)

def low_pass(kept, grad):
    return (grad,)

def back_keep(v):
    return (v, None)

def back_low(kept, grad):
    return (low(grad),)
low.defvjp(low_keep, low_pass)
low_back.defvjp(back_keep, back_low)
EPS = 1e-05
MASKED = -1e+30
HIGHEST = lax.Precision.HIGHEST

def layer_norm(inputs, gain_row, bias_term):
    center = lax.optimization_barrier(jnp.mean(inputs, axis=-1, keepdims=True))
    offset = inputs - center
    spread = lax.optimization_barrier(jnp.mean(offset * offset, axis=-1, keepdims=True))
    return offset * lax.rsqrt(spread + EPS) * gain_row + bias_term

def rounded_both(inputs):
    return low(low_back(inputs))

def exact_dot(former, latter):
    return jnp.dot(former, latter, precision=HIGHEST)

def split_heads(inputs):
    return inputs.reshape(inputs.shape[0] // ROW, ROW, HEADS, HEAD_DIM)

def layer_block(weights, token_rows, cond_rows):
    gain_one, bias_one, qkv_mat, query_add, value_add, out_mat, out_add, gain_two, bias_two, fc_mat, fc_add, proj_mat, proj_add = [low(member) for member in weights]
    base_rows = token_rows + cond_rows
    first_normed = low(layer_norm(base_rows, gain_one, bias_one))
    joined = exact_dot(first_normed, qkv_mat)
    queries = rounded_both(joined[:, :D] + query_add)
    key_rows = rounded_both(joined[:, D:2 * D])
    values = rounded_both(joined[:, 2 * D:] + value_add)
    factor = HEAD_DIM ** (-0.5)
    scores = low_back(jnp.einsum('bqhe,bkhe->bhqk', split_heads(queries), split_heads(key_rows), precision=HIGHEST) * factor)
    places = jnp.arange(ROW, dtype=jnp.int32)
    scores = jnp.where((places[:, None] >= places[None, :])[None, None], scores, MASKED)
    row_max = lax.optimization_barrier(jnp.max(scores, axis=-1, keepdims=True))
    powers = jnp.exp(scores - row_max)
    probs_low = low(powers / lax.optimization_barrier(jnp.sum(powers, axis=-1, keepdims=True)))
    mixed = jnp.einsum('bhqk,bkhe->bqhe', probs_low, split_heads(values), precision=HIGHEST)
    mixed_rows = rounded_both(mixed.reshape(token_rows.shape))
    middle = base_rows + low_back(exact_dot(mixed_rows, out_mat) + out_add)
    second_normed = low(layer_norm(middle, gain_two, bias_two))
    hidden_pre = low_back(exact_dot(second_normed, fc_mat) + fc_add)
    hidden = low(jax.nn.gelu(hidden_pre, approximate=True))
    return middle + low_back(exact_dot(hidden, proj_mat) + proj_add)

def reference(layer_input, cond_table, window_bucket, window_blocks, cotangent, ln1_gain, ln1_bias, qkv_weight, query_bias, value_bias, out_weight, out_bias, ln2_gain, ln2_bias, fc_weight, fc_bias, proj_weight, proj_bias):
    params = (ln1_gain, ln1_bias, qkv_weight, query_bias, value_bias, out_weight, out_bias, ln2_gain, ln2_bias, fc_weight, fc_bias, proj_weight, proj_bias)
    cond_rows = cond_table.astype(jnp.float32)[window_bucket]
    places = jnp.arange(LEN, dtype=jnp.int32) // ROW
    keep_mask = (places[None, :] < window_blocks[:, None]).astype(jnp.float32)
    groups = WINDOWS // 2
    inputs = layer_input.astype(jnp.float32).reshape(groups, 2 * LEN, D)
    conds = jnp.broadcast_to(cond_rows[:, None, :], (WINDOWS, LEN, D)).reshape(groups, 2 * LEN, D)
    grads_in = (cotangent.astype(jnp.float32) * keep_mask[:, :, None]).reshape(groups, 2 * LEN, D)
    starting = tuple((jnp.zeros_like(member) for member in params))

    def scan_step(running, scan_item):
        block_in, cond_in, grad_in = scan_item

        def applied(weights, token_rows):
            return layer_block(weights, token_rows, cond_in)
        output, pullback = jax.vjp(applied, params, block_in)
        grad_params, grad_rows = pullback(grad_in)
        running = tuple((former + addend for former, addend in zip(running, grad_params)))
        return (running, (output.astype(jnp.bfloat16), grad_rows))
    totals, (outputs, grads) = lax.scan(scan_step, starting, (inputs, conds, grads_in))
    return (outputs.reshape(WINDOWS, LEN, D), grads.reshape(WINDOWS, LEN, D), totals[0], totals[1], totals[2], totals[3], totals[4], totals[5], totals[6], totals[7], totals[8], totals[9], totals[10], totals[11], totals[12])
```

```python
import jax
import jax.numpy as jnp
from jax import lax
from jax.sharding import PartitionSpec as P

HEADS = 16
HEAD_DIM = 64
ROW = 128


EPS = 1e-05
MASKED = -1e30


def layer_norm(inputs, gain_row, bias_term):
    center = jnp.mean(inputs, axis=-1, keepdims=True)
    offset = inputs - center
    spread = jnp.mean(offset * offset, axis=-1, keepdims=True)
    return offset * lax.rsqrt(spread + EPS) * gain_row + bias_term


def norm_backward(inputs, gain_row, bias_term, upstream):
    result, pullback = jax.vjp(layer_norm, inputs, gain_row, bias_term)
    return pullback(upstream)


def gelu_tanh(inputs):
    return jax.nn.gelu(inputs, approximate=True)


def column_sum(inputs):
    return jnp.sum(inputs.astype(jnp.float32), axis=0)


def cross_rows(former, latter):
    return lax.dot_general(
        former, latter, (((0,), (0,)), ((), ())), preferred_element_type=jnp.float32
    )


def times_transposed(former, latter):
    return lax.dot_general(
        former, latter, (((1,), (1,)), ((), ())), preferred_element_type=jnp.float32
    )


def split_heads(inputs):
    return inputs.reshape(inputs.shape[0] // ROW, ROW, HEADS, HEAD_DIM)


def block_scores(queries, key_rows):
    factor = HEAD_DIM ** (-0.5)
    scores = (
        jnp.einsum(
            "bqhe,bkhe->bhqk",
            split_heads(queries),
            split_heads(key_rows),
            preferred_element_type=jnp.float32,
        )
        * factor
    )
    places = jnp.arange(ROW, dtype=jnp.int32)
    return jnp.where((places[:, None] >= places[None, :])[None, None], scores, MASKED)


def project(normed, weights, query_add, value_add):
    features = normed.shape[1]
    joined = jnp.dot(normed, weights, preferred_element_type=jnp.float32)
    queries = (joined[:, :features] + query_add).astype(jnp.bfloat16)
    key_rows = joined[:, features : 2 * features].astype(jnp.bfloat16)
    values = (joined[:, 2 * features :] + value_add).astype(jnp.bfloat16)
    return (queries, key_rows, values)


def attention_forward(queries, key_rows, values):
    scores = block_scores(queries, key_rows)
    row_max = jnp.max(scores, axis=-1, keepdims=True)
    powers = jnp.exp(scores - row_max)
    totals = jnp.sum(powers, axis=-1, keepdims=True)
    probs_low = (powers / totals).astype(jnp.bfloat16)
    mixed = jnp.einsum(
        "bhqk,bkhe->bqhe", probs_low, split_heads(values), preferred_element_type=jnp.float32
    )
    return (mixed.reshape(queries.shape).astype(jnp.bfloat16), row_max + jnp.log(totals))


def attention_backward(queries, key_rows, values, log_total, grad_mixed):
    factor = HEAD_DIM ** (-0.5)
    softmax_rows = jnp.exp(block_scores(queries, key_rows) - log_total)
    probs_low = softmax_rows.astype(jnp.bfloat16)
    grad_heads = split_heads(grad_mixed)
    grad_probs = jnp.einsum(
        "bqhe,bkhe->bhqk", grad_heads, split_heads(values), preferred_element_type=jnp.float32
    )
    grad_values = jnp.einsum(
        "bhqk,bqhe->bkhe", probs_low, grad_heads, preferred_element_type=jnp.float32
    )
    weighted = jnp.sum(grad_probs * softmax_rows, axis=-1, keepdims=True)
    grad_scores = (softmax_rows * (grad_probs - weighted)).astype(jnp.bfloat16)
    grad_queries = (
        jnp.einsum(
            "bhqk,bkhe->bqhe",
            grad_scores,
            split_heads(key_rows),
            preferred_element_type=jnp.float32,
        )
        * factor
    )
    grad_keys = (
        jnp.einsum(
            "bhqk,bqhe->bkhe", grad_scores, split_heads(queries), preferred_element_type=jnp.float32
        )
        * factor
    )
    row_shape = queries.shape
    return jnp.concatenate(
        [
            grad_queries.reshape(row_shape),
            grad_keys.reshape(row_shape),
            grad_values.reshape(row_shape),
        ],
        axis=1,
    ).astype(jnp.bfloat16)


AXES = ("dp", "seq", "shard")


def gather_all(members):
    devices = lax.psum(1, AXES)
    flat = jnp.concatenate([member for member in members if member.ndim == 1])
    joined = lax.all_gather(flat, AXES, axis=0, tiled=False)
    results = []
    start = 0
    for member in members:
        if member.ndim == 1:
            size = member.shape[0]
            results.append(joined[:, start : start + size].reshape(devices * size))
            start += size
        else:
            results.append(lax.all_gather(member, AXES, axis=0, tiled=True))
    return tuple(results)


def scatter_all(members):
    devices = lax.psum(1, AXES)
    flat = jnp.concatenate(
        [member.reshape(devices, -1) for member in members if member.ndim == 1], axis=1
    )
    summed = lax.psum_scatter(flat, AXES, scatter_dimension=0, tiled=False)
    results = []
    start = 0
    for member in members:
        if member.ndim == 1:
            size = member.shape[0] // devices
            results.append(summed[start : start + size])
            start += size
        else:
            share = lax.psum_scatter(
                member.astype(jnp.bfloat16), AXES, scatter_dimension=0, tiled=True
            )
            results.append(share.astype(jnp.float32))
    return tuple(results)


def on_device(
    layer_input,
    cond_table,
    window_bucket,
    window_blocks,
    cotangent,
    ln1_gain,
    ln1_bias,
    qkv_weight,
    query_bias,
    value_bias,
    out_weight,
    out_bias,
    ln2_gain,
    ln2_bias,
    fc_weight,
    fc_bias,
    proj_weight,
    proj_bias,
):
    masters = (
        ln1_gain,
        ln1_bias,
        qkv_weight,
        query_bias,
        value_bias,
        out_weight,
        out_bias,
        ln2_gain,
        ln2_bias,
        fc_weight,
        fc_bias,
        proj_weight,
        proj_bias,
    )
    lowered = [member.astype(jnp.bfloat16) for member in masters]
    gathered = gather_all(lowered)
    floats = [member.astype(jnp.float32) for member in gathered]
    windows, window_span, features = layer_input.shape
    buckets = jnp.arange(cond_table.shape[0], dtype=jnp.int32)
    one_hot = (window_bucket[:, None] == buckets[None, :]).astype(jnp.float32)
    cond_rows = jnp.dot(one_hot, cond_table.astype(jnp.float32), precision=lax.Precision.HIGHEST)
    base_rows = (layer_input.astype(jnp.float32) + cond_rows[:, None, :]).reshape(
        windows * window_span, features
    )
    first_normed = layer_norm(base_rows, floats[0], floats[1]).astype(jnp.bfloat16)
    queries, key_rows, values = project(first_normed, gathered[2], floats[3], floats[4])
    mixed_rows, log_total = attention_forward(queries, key_rows, values)
    middle = (
        base_rows + jnp.dot(mixed_rows, gathered[5], preferred_element_type=jnp.float32) + floats[6]
    )
    second_normed = layer_norm(middle, floats[7], floats[8]).astype(jnp.bfloat16)
    hidden_pre = (
        jnp.dot(second_normed, gathered[9], preferred_element_type=jnp.float32) + floats[10]
    )
    hidden = gelu_tanh(hidden_pre).astype(jnp.bfloat16)
    final_rows = (
        middle + jnp.dot(hidden, gathered[11], preferred_element_type=jnp.float32) + floats[12]
    )
    layer_output = final_rows.astype(jnp.bfloat16).reshape(windows, window_span, features)
    back_params = gathered
    back_floats = [member.astype(jnp.float32) for member in back_params]
    first_place = lax.axis_index("seq") * window_span
    places = first_place + jnp.arange(window_span, dtype=jnp.int32)
    keep_mask = (places[None, :] // ROW < window_blocks[:, None]).astype(jnp.float32)
    grad_out = (cotangent.astype(jnp.float32) * keep_mask[:, :, None]).reshape(
        windows * window_span, features
    )
    grad_low = grad_out.astype(jnp.bfloat16)
    proj_w_grad = cross_rows(hidden, grad_low)
    proj_b_grad = column_sum(grad_out)
    grad_hidden = times_transposed(grad_low, back_params[11])
    gelu_value, gelu_pull = jax.vjp(gelu_tanh, hidden_pre)
    grad_pre = gelu_pull(grad_hidden)[0].astype(jnp.bfloat16)
    fc_w_grad = cross_rows(second_normed, grad_pre)
    fc_b_grad = column_sum(grad_pre)
    grad_second = times_transposed(grad_pre, back_params[9])
    grad_middle_norm, ln2_g_grad, ln2_b_grad = norm_backward(
        middle, back_floats[7], back_floats[8], grad_second
    )
    grad_middle = grad_out + grad_middle_norm
    grad_branch = grad_middle.astype(jnp.bfloat16)
    out_w_grad = cross_rows(mixed_rows, grad_branch)
    out_b_grad = column_sum(grad_branch)
    grad_mixed = times_transposed(grad_branch, back_params[5]).astype(jnp.bfloat16)
    again_normed = layer_norm(base_rows, back_floats[0], back_floats[1]).astype(jnp.bfloat16)
    again_queries, again_keys, again_values = project(
        again_normed, back_params[2], back_floats[3], back_floats[4]
    )
    grad_qkv = attention_backward(again_queries, again_keys, again_values, log_total, grad_mixed)
    qkv_w_grad = cross_rows(again_normed, grad_qkv)
    query_b_grad = column_sum(grad_qkv[:, :features])
    value_b_grad = column_sum(grad_qkv[:, 2 * features :])
    grad_first = times_transposed(grad_qkv, back_params[2])
    grad_base_norm, ln1_g_grad, ln1_b_grad = norm_backward(
        base_rows, back_floats[0], back_floats[1], grad_first
    )
    input_grad = (grad_middle + grad_base_norm).reshape(windows, window_span, features)
    shares = scatter_all(
        (
            ln1_g_grad,
            ln1_b_grad,
            qkv_w_grad,
            query_b_grad,
            value_b_grad,
            out_w_grad,
            out_b_grad,
            ln2_g_grad,
            ln2_b_grad,
            fc_w_grad,
            fc_b_grad,
            proj_w_grad,
            proj_b_grad,
        )
    )
    return (
        layer_output,
        input_grad,
        shares[0],
        shares[1],
        shares[2],
        shares[3],
        shares[4],
        shares[5],
        shares[6],
        shares[7],
        shares[8],
        shares[9],
        shares[10],
        shares[11],
        shares[12],
    )


def solution(mesh):
    placed = (
        P(("dp", "shard"), "seq", None),
        P(),
        P(("dp", "shard")),
        P(("dp", "shard")),
        P(("dp", "shard"), "seq", None),
        P(("dp", "seq", "shard")),
        P(("dp", "seq", "shard")),
        P(("dp", "seq", "shard"), None),
        P(("dp", "seq", "shard")),
        P(("dp", "seq", "shard")),
        P(("dp", "seq", "shard"), None),
        P(("dp", "seq", "shard")),
        P(("dp", "seq", "shard")),
        P(("dp", "seq", "shard")),
        P(("dp", "seq", "shard"), None),
        P(("dp", "seq", "shard")),
        P(("dp", "seq", "shard"), None),
        P(("dp", "seq", "shard")),
    )
    return jax.shard_map(
        on_device,
        mesh=mesh,
        in_specs=placed,
        out_specs=(
            P(("dp", "shard"), "seq", None),
            P(("dp", "shard"), "seq", None),
            P(("dp", "seq", "shard")),
            P(("dp", "seq", "shard")),
            P(("dp", "seq", "shard"), None),
            P(("dp", "seq", "shard")),
            P(("dp", "seq", "shard")),
            P(("dp", "seq", "shard"), None),
            P(("dp", "seq", "shard")),
            P(("dp", "seq", "shard")),
            P(("dp", "seq", "shard")),
            P(("dp", "seq", "shard"), None),
            P(("dp", "seq", "shard")),
            P(("dp", "seq", "shard"), None),
            P(("dp", "seq", "shard")),
        ),
        check_vma=False,
    )
```

```python
import jax
import jax.numpy as jnp
from jax import lax
from jax.sharding import PartitionSpec as P

HEADS = 16
HEAD_DIM = 64
ROW = 128


EPS = 1e-05
MASKED = -1e30


def layer_norm(inputs, gain_row, bias_term):
    center = jnp.mean(inputs, axis=-1, keepdims=True)
    offset = inputs - center
    spread = jnp.mean(offset * offset, axis=-1, keepdims=True)
    return offset * lax.rsqrt(spread + EPS) * gain_row + bias_term


def norm_backward(inputs, gain_row, bias_term, upstream):
    result, pullback = jax.vjp(layer_norm, inputs, gain_row, bias_term)
    return pullback(upstream)


def gelu_tanh(inputs):
    return jax.nn.gelu(inputs, approximate=True)


def column_sum(inputs):
    return jnp.sum(inputs.astype(jnp.float32), axis=0)


def cross_rows(former, latter):
    return lax.dot_general(
        former, latter, (((0,), (0,)), ((), ())), preferred_element_type=jnp.float32
    )


def times_transposed(former, latter):
    return lax.dot_general(
        former, latter, (((1,), (1,)), ((), ())), preferred_element_type=jnp.float32
    )


def split_heads(inputs):
    return inputs.reshape(inputs.shape[0] // ROW, ROW, HEADS, HEAD_DIM)


def block_scores(queries, key_rows):
    factor = HEAD_DIM ** (-0.5)
    scores = (
        jnp.einsum(
            "bqhe,bkhe->bhqk",
            split_heads(queries),
            split_heads(key_rows),
            preferred_element_type=jnp.float32,
        )
        * factor
    )
    places = jnp.arange(ROW, dtype=jnp.int32)
    return jnp.where((places[:, None] >= places[None, :])[None, None], scores, MASKED)


def project(normed, weights, query_add, value_add):
    features = normed.shape[1]
    joined = jnp.dot(normed, weights, preferred_element_type=jnp.float32)
    queries = (joined[:, :features] + query_add).astype(jnp.bfloat16)
    key_rows = joined[:, features : 2 * features].astype(jnp.bfloat16)
    values = (joined[:, 2 * features :] + value_add).astype(jnp.bfloat16)
    return (queries, key_rows, values)


def attention_forward(queries, key_rows, values):
    scores = block_scores(queries, key_rows)
    row_max = jnp.max(scores, axis=-1, keepdims=True)
    powers = jnp.exp(scores - row_max)
    totals = jnp.sum(powers, axis=-1, keepdims=True)
    probs_low = (powers / totals).astype(jnp.bfloat16)
    mixed = jnp.einsum(
        "bhqk,bkhe->bqhe", probs_low, split_heads(values), preferred_element_type=jnp.float32
    )
    return (mixed.reshape(queries.shape).astype(jnp.bfloat16), row_max + jnp.log(totals))


def attention_backward(queries, key_rows, values, log_total, grad_mixed):
    factor = HEAD_DIM ** (-0.5)
    softmax_rows = jnp.exp(block_scores(queries, key_rows) - log_total)
    probs_low = softmax_rows.astype(jnp.bfloat16)
    grad_heads = split_heads(grad_mixed)
    grad_probs = jnp.einsum(
        "bqhe,bkhe->bhqk", grad_heads, split_heads(values), preferred_element_type=jnp.float32
    )
    grad_values = jnp.einsum(
        "bhqk,bqhe->bkhe", probs_low, grad_heads, preferred_element_type=jnp.float32
    )
    weighted = jnp.sum(grad_probs * softmax_rows, axis=-1, keepdims=True)
    grad_scores = (softmax_rows * (grad_probs - weighted)).astype(jnp.bfloat16)
    grad_queries = (
        jnp.einsum(
            "bhqk,bkhe->bqhe",
            grad_scores,
            split_heads(key_rows),
            preferred_element_type=jnp.float32,
        )
        * factor
    )
    grad_keys = (
        jnp.einsum(
            "bhqk,bqhe->bkhe", grad_scores, split_heads(queries), preferred_element_type=jnp.float32
        )
        * factor
    )
    row_shape = queries.shape
    return jnp.concatenate(
        [
            grad_queries.reshape(row_shape),
            grad_keys.reshape(row_shape),
            grad_values.reshape(row_shape),
        ],
        axis=1,
    ).astype(jnp.bfloat16)


AXES = ("dp", "seq", "shard")


def gather_all(members):
    devices = lax.psum(1, AXES)
    flat = jnp.concatenate([member for member in members if member.ndim == 1])
    joined = lax.all_gather(flat, AXES, axis=0, tiled=False)
    results = []
    start = 0
    for member in members:
        if member.ndim == 1:
            size = member.shape[0]
            results.append(joined[:, start : start + size].reshape(devices * size))
            start += size
        else:
            results.append(lax.all_gather(member, AXES, axis=0, tiled=True))
    return tuple(results)


def staged_scatter(member):
    share = member
    for name in AXES:
        share = lax.psum_scatter(share, name, scatter_dimension=0, tiled=True)
    return share


def scatter_all(members):
    devices = lax.psum(1, AXES)
    flat = jnp.concatenate(
        [member.reshape(devices, -1) for member in members if member.ndim == 1], axis=1
    )
    summed = lax.psum_scatter(flat, AXES, scatter_dimension=0, tiled=False)
    results = []
    start = 0
    for member in members:
        if member.ndim == 1:
            size = member.shape[0] // devices
            results.append(summed[start : start + size])
            start += size
        else:
            share = staged_scatter(member.astype(jnp.bfloat16))
            results.append(share.astype(jnp.float32))
    return tuple(results)


def on_device(
    layer_input,
    cond_table,
    window_bucket,
    window_blocks,
    cotangent,
    ln1_gain,
    ln1_bias,
    qkv_weight,
    query_bias,
    value_bias,
    out_weight,
    out_bias,
    ln2_gain,
    ln2_bias,
    fc_weight,
    fc_bias,
    proj_weight,
    proj_bias,
):
    masters = (
        ln1_gain,
        ln1_bias,
        qkv_weight,
        query_bias,
        value_bias,
        out_weight,
        out_bias,
        ln2_gain,
        ln2_bias,
        fc_weight,
        fc_bias,
        proj_weight,
        proj_bias,
    )
    lowered = [member.astype(jnp.bfloat16) for member in masters]
    gathered = gather_all(lowered)
    floats = [member.astype(jnp.float32) for member in gathered]
    windows, window_span, features = layer_input.shape
    buckets = jnp.arange(cond_table.shape[0], dtype=jnp.int32)
    one_hot = (window_bucket[:, None] == buckets[None, :]).astype(jnp.float32)
    cond_rows = jnp.dot(one_hot, cond_table.astype(jnp.float32), precision=lax.Precision.HIGHEST)
    base_rows = (layer_input.astype(jnp.float32) + cond_rows[:, None, :]).reshape(
        windows * window_span, features
    )
    first_normed = layer_norm(base_rows, floats[0], floats[1]).astype(jnp.bfloat16)
    queries, key_rows, values = project(first_normed, gathered[2], floats[3], floats[4])
    mixed_rows, log_total = attention_forward(queries, key_rows, values)
    middle = (
        base_rows + jnp.dot(mixed_rows, gathered[5], preferred_element_type=jnp.float32) + floats[6]
    )
    second_normed = layer_norm(middle, floats[7], floats[8]).astype(jnp.bfloat16)
    hidden_pre = (
        jnp.dot(second_normed, gathered[9], preferred_element_type=jnp.float32) + floats[10]
    )
    hidden = gelu_tanh(hidden_pre).astype(jnp.bfloat16)
    final_rows = (
        middle + jnp.dot(hidden, gathered[11], preferred_element_type=jnp.float32) + floats[12]
    )
    layer_output = final_rows.astype(jnp.bfloat16).reshape(windows, window_span, features)
    back_params = gathered
    back_floats = [member.astype(jnp.float32) for member in back_params]
    first_place = lax.axis_index("seq") * window_span
    places = first_place + jnp.arange(window_span, dtype=jnp.int32)
    keep_mask = (places[None, :] // ROW < window_blocks[:, None]).astype(jnp.float32)
    grad_out = (cotangent.astype(jnp.float32) * keep_mask[:, :, None]).reshape(
        windows * window_span, features
    )
    grad_low = grad_out.astype(jnp.bfloat16)
    proj_w_grad = cross_rows(hidden, grad_low)
    proj_b_grad = column_sum(grad_out)
    grad_hidden = times_transposed(grad_low, back_params[11])
    gelu_value, gelu_pull = jax.vjp(gelu_tanh, hidden_pre)
    grad_pre = gelu_pull(grad_hidden)[0].astype(jnp.bfloat16)
    fc_w_grad = cross_rows(second_normed, grad_pre)
    fc_b_grad = column_sum(grad_pre)
    grad_second = times_transposed(grad_pre, back_params[9])
    grad_middle_norm, ln2_g_grad, ln2_b_grad = norm_backward(
        middle, back_floats[7], back_floats[8], grad_second
    )
    grad_middle = grad_out + grad_middle_norm
    grad_branch = grad_middle.astype(jnp.bfloat16)
    out_w_grad = cross_rows(mixed_rows, grad_branch)
    out_b_grad = column_sum(grad_branch)
    grad_mixed = times_transposed(grad_branch, back_params[5]).astype(jnp.bfloat16)
    again_normed = layer_norm(base_rows, back_floats[0], back_floats[1]).astype(jnp.bfloat16)
    again_queries, again_keys, again_values = project(
        again_normed, back_params[2], back_floats[3], back_floats[4]
    )
    grad_qkv = attention_backward(again_queries, again_keys, again_values, log_total, grad_mixed)
    qkv_w_grad = cross_rows(again_normed, grad_qkv)
    query_b_grad = column_sum(grad_qkv[:, :features])
    value_b_grad = column_sum(grad_qkv[:, 2 * features :])
    grad_first = times_transposed(grad_qkv, back_params[2])
    grad_base_norm, ln1_g_grad, ln1_b_grad = norm_backward(
        base_rows, back_floats[0], back_floats[1], grad_first
    )
    input_grad = (grad_middle + grad_base_norm).reshape(windows, window_span, features)
    shares = scatter_all(
        (
            ln1_g_grad,
            ln1_b_grad,
            qkv_w_grad,
            query_b_grad,
            value_b_grad,
            out_w_grad,
            out_b_grad,
            ln2_g_grad,
            ln2_b_grad,
            fc_w_grad,
            fc_b_grad,
            proj_w_grad,
            proj_b_grad,
        )
    )
    return (
        layer_output,
        input_grad,
        shares[0],
        shares[1],
        shares[2],
        shares[3],
        shares[4],
        shares[5],
        shares[6],
        shares[7],
        shares[8],
        shares[9],
        shares[10],
        shares[11],
        shares[12],
    )


def solution(mesh):
    placed = (
        P(("dp", "shard"), "seq", None),
        P(),
        P(("dp", "shard")),
        P(("dp", "shard")),
        P(("dp", "shard"), "seq", None),
        P(("dp", "seq", "shard")),
        P(("dp", "seq", "shard")),
        P(("dp", "seq", "shard"), None),
        P(("dp", "seq", "shard")),
        P(("dp", "seq", "shard")),
        P(("dp", "seq", "shard"), None),
        P(("dp", "seq", "shard")),
        P(("dp", "seq", "shard")),
        P(("dp", "seq", "shard")),
        P(("dp", "seq", "shard"), None),
        P(("dp", "seq", "shard")),
        P(("dp", "seq", "shard"), None),
        P(("dp", "seq", "shard")),
    )
    return jax.shard_map(
        on_device,
        mesh=mesh,
        in_specs=placed,
        out_specs=(
            P(("dp", "shard"), "seq", None),
            P(("dp", "shard"), "seq", None),
            P(("dp", "seq", "shard")),
            P(("dp", "seq", "shard")),
            P(("dp", "seq", "shard"), None),
            P(("dp", "seq", "shard")),
            P(("dp", "seq", "shard")),
            P(("dp", "seq", "shard"), None),
            P(("dp", "seq", "shard")),
            P(("dp", "seq", "shard")),
            P(("dp", "seq", "shard")),
            P(("dp", "seq", "shard"), None),
            P(("dp", "seq", "shard")),
            P(("dp", "seq", "shard"), None),
            P(("dp", "seq", "shard")),
        ),
        check_vma=False,
    )
```
